128 devices in a mesh: dp: 8 (over x, core), ctx: 16 (over z, y).
Axes of the slice: x: 4, y: 4, z: 4, core: 2. Of those that a mesh axis runs over, the one named last changes fastest.
Arguments:
- queries: bfloat16 [8, 2048, 2048], P('dp', 'ctx'), may hold values from -6 to 6
- keys: bfloat16 [8, 2048, 2048], P('dp', 'ctx'), may hold values from -6 to 6
- values: bfloat16 [8, 2048, 2048], P('dp', 'ctx'), may hold values from -6 to 6
- cotangent: bfloat16 [8, 2048, 2048], P('dp', 'ctx'), may hold values from -6 to 6
- doc_lengths: int32 [8, 4], P('dp'), may hold values from 0 to 2048, as said below
- filter_taps: float32 [2048, 2048], P('ctx'), may hold values from -0.13258252 to 0.13258252
Outputs:
- hyena_out: bfloat16 [8, 2048, 2048], P('dp', 'ctx')
- grad_queries: bfloat16 [8, 2048, 2048], P('dp', 'ctx')
- grad_keys: bfloat16 [8, 2048, 2048], P('dp', 'ctx')
- grad_values: bfloat16 [8, 2048, 2048], P('dp', 'ctx')
- grad_filter: float32 [2048, 2048], P('ctx', 'dp')
The draws below stay inside these ranges and needn't reach their ends.
Inputs may be any that keep to these rules, and one draw needn't show every extreme that they name: `doc_lengths`: each row holds 4 document lengths that sum to 2048; a length may be zero (an unused slot); in every draw some row holds a single document of all 2048 positions.
All inputs are finite; a program needn't handle non-finite values.
Results may differ from the reference program's by a relative error of at most 0.0051.
Values may be sent and summed in bfloat16 or wider, within the bound.
No kernel may reach another device: no remote copies, remote signals or barrier semaphores. Data moves between devices by JAX's collectives and lax.ppermute only.
A program may use at most 512 MiB of HBM per device.

```python
import jax
import jax.numpy as jnp
from jax import lax

D = 2048
DOCS = 4
SEQ = 2048
BATCH = 8


def draw_doc_lengths(key, part):
    cut_key = jax.random.fold_in(key, 11)
    row_key = jax.random.fold_in(key, 23)
    cut_points = jnp.sort(jax.random.randint(cut_key, (BATCH, DOCS - 1), 0, SEQ + 1), axis=1).astype(jnp.int32)
    whole_row = jax.random.randint(row_key, (), 0, BATCH).astype(jnp.int32)
    row_index = lax.broadcasted_iota(jnp.int32, (BATCH, DOCS - 1), 0)
    cut_points = jnp.where(row_index == whole_row, SEQ, cut_points).astype(jnp.int32)
    bounds = jnp.concatenate([jnp.zeros((BATCH, 1), jnp.int32), cut_points, jnp.full((BATCH, 1), SEQ, jnp.int32)], axis=1)
    return (bounds[:, 1:] - bounds[:, :-1]).astype(jnp.int32)


def with_spikes(drawn, key, source, target, shards_of, factor):
    def block_of(axis_at):
        return (jnp.arange(drawn.shape[axis_at]) // (drawn.shape[axis_at] // shards_of)).reshape((-1,) + (1,) * (drawn.ndim - 1 - axis_at))

    first = jax.random.permutation(key, shards_of)[block_of(target)]
    second = (block_of(target) + shards_of // 2) % shards_of
    return jnp.where((block_of(source) == first) | (block_of(source) == second), factor * drawn, drawn)


def block_scale(key, dims, cuts, low, top_value):
    loudness, own = 1.0, jax.random.fold_in(key, 6)
    for axis_at, parts in cuts:
        steps = jnp.exp(jax.random.uniform(jax.random.fold_in(own, axis_at), (parts,), jnp.float32, low / len(cuts), top_value / len(cuts)))
        loudness = loudness * jnp.repeat(steps, dims[axis_at] // parts).reshape([-1 if axis == axis_at else 1 for axis in range(len(dims))])
    return loudness


def scatter_about(rng, dims, deviation, reach, shards=(), kind=jnp.bfloat16):
    loudness = block_scale(rng, dims, shards, -0.22, 0.18) if shards else 1.0
    values = jax.random.normal(rng, dims, jnp.float32) * deviation * loudness
    return jnp.minimum(jnp.maximum(values, -reach), reach).astype(kind)


def heavy_noise(rng, extent, spread, limit, split, heavy, kind=jnp.bfloat16):
    values = spread * jax.random.normal(rng, extent, jnp.float32)
    if split:
        values = values * block_scale(rng, extent, split, -0.22, 0.18)
    return jnp.clip(with_spikes(values, jax.random.fold_in(rng, 3), *heavy), -limit, limit).astype(kind)


def setup_inputs(seed: int = 0) -> dict:
    seeds = jax.random.split(jax.random.key(seed), 7)
    return {
        "queries": scatter_about(seeds[0], (BATCH, SEQ, D), 1.0, 6.0, ((0, 8), (1, 16))),
        "keys": scatter_about(seeds[1], (BATCH, SEQ, D), 1.0, 6.0, ((0, 8), (1, 16))),
        "values": scatter_about(seeds[2], (BATCH, SEQ, D), 1.0, 6.0, ((0, 8), (1, 16))),
        "cotangent": heavy_noise(seeds[3], (BATCH, SEQ, D), 1.0, 6.0, ((0, 8), (1, 16)), (0, 2, 8, 2.0)),
        "doc_lengths": draw_doc_lengths(jax.random.fold_in(seeds[6], 71), 0),
        "filter_taps": scatter_about(seeds[5], (SEQ, D), (SEQ ** -0.5), 0.13258252, ((0, 16),), jnp.float32),
    }


def document_ids(lengths, count):
    doc_ends = jnp.cumsum(lengths)
    positions = jnp.arange(count, dtype=jnp.int32)
    return lax.optimization_barrier(jnp.sum((doc_ends[None, :] <= positions[:, None]).astype(jnp.int32), axis=1))

def reset_convolution(filter_taps, signal, doc_of):
    period = 2 * signal.shape[0]
    filter_freq = jnp.fft.rfft(filter_taps, period, axis=0)
    total = jnp.zeros_like(signal)
    for doc_index in range(DOCS):
        keep_col = (doc_of == doc_index).astype(signal.dtype)[:, None]
        spectrum = filter_freq * jnp.fft.rfft(keep_col * signal, period, axis=0)
        part_conv = jnp.fft.irfft(spectrum, period, axis=0)[:signal.shape[0]]
        total = total + keep_col * part_conv
    return total

def reference(queries, keys, values, cotangent, doc_lengths, filter_taps):

    def one_sequence(grad_sum, inputs):
        query_row, key_row, value_row, cot_row, length_row = inputs
        doc_of = document_ids(length_row, SEQ)
        query_f = query_row.astype(jnp.float32)
        key_f = key_row.astype(jnp.float32)
        value_f = value_row.astype(jnp.float32)
        cot_f = cot_row.astype(jnp.float32)
        gated = lax.optimization_barrier((key_f * value_f).astype(jnp.bfloat16)).astype(jnp.float32)
        conv_out, pullback = jax.vjp(lambda taps, signal: reset_convolution(taps, signal, doc_of), filter_taps, gated)
        weighted = lax.optimization_barrier((cot_f * query_f).astype(jnp.bfloat16)).astype(jnp.float32)
        grad_taps, grad_signal = pullback(weighted)
        outputs = ((query_f * conv_out).astype(jnp.bfloat16), (cot_f * conv_out).astype(jnp.bfloat16), (grad_signal * value_f).astype(jnp.bfloat16), (grad_signal * key_f).astype(jnp.bfloat16))
        return (grad_sum + grad_taps, outputs)
    grad_total, outputs = lax.scan(one_sequence, jnp.zeros_like(filter_taps), (queries, keys, values, cotangent, doc_lengths))
    return (outputs[0], outputs[1], outputs[2], outputs[3], grad_total)
```

```python
import functools

import jax
import jax.numpy as jnp
from jax import lax
from jax.experimental import pallas as pl
from jax.experimental.pallas import tpu as pltpu
from jax.sharding import PartitionSpec as P

BLOCK = 128
SEQS = 8
BLOCKS = 16
PEERS = SEQS * BLOCKS
OWN = 16
DOCS = 4
ROWS = 40
FILT, DOC = 2 * OWN, 2 * OWN + 2
F32, BF16 = jnp.float32, jnp.bfloat16


def iota(axis, shape=(BLOCK, BLOCK)):
    return lax.broadcasted_iota(jnp.int32, shape, axis)


def dot(a, b):
    return jnp.dot(a, b, preferred_element_type=F32)


def dot_nt(a, b):
    return lax.dot_general(a, b, (((1,), (1,)), ((), ())), preferred_element_type=F32)


def eye_rev():
    row, col = iota(0), iota(1)
    return (row == col).astype(F32).astype(BF16), (row + col == BLOCK - 1).astype(F32).astype(BF16)


def put(ref, start, stride, tile):
    for r in range(tile.shape[0] // 8):
        ref[pl.ds(start + r * 8 * stride, 8, stride=stride), :] = tile[8 * r : 8 * r + 8]


def take(ref, start, stride, rows):
    return jnp.concatenate(
        [ref[pl.ds(start + r * 8 * stride, 8, stride=stride), :] for r in range(rows // 8)], axis=0
    )


def pack_kernel(len_ref, q_ref, k_ref, v_ref, c_ref, filt_hbm, out_ref, stage, filt, sem):
    step = pl.program_id(0)
    tiles = q_ref.shape[2] // BLOCK
    eye, rev = eye_rev()
    copy = pltpu.make_async_copy(
        filt_hbm.at[:, pl.ds(pl.multiple_of(lax.axis_index("dp") * 2 * BLOCK, BLOCK), 2 * BLOCK)],
        filt,
        sem,
    )

    @pl.when(step == 0)
    def _():
        copy.start()
        lane = iota(1, (8, BLOCK))
        pos = lax.axis_index("ctx") * BLOCK + lane
        pos_rev = lax.axis_index("ctx") * BLOCK + BLOCK - 1 - lane
        doc = jnp.zeros((8, BLOCK), F32)
        doc_rev = jnp.zeros((8, BLOCK), F32)
        end = jnp.int32(0)
        for i in range(DOCS):
            end = end + len_ref[0, i]
            doc = doc + (end <= pos).astype(F32)
            doc_rev = doc_rev + (end <= pos_rev).astype(F32)
        zero = jnp.zeros((8, BLOCK), F32)
        for r in range(PEERS // 8):
            put(stage, DOC + r * 8 * ROWS, ROWS, doc)
            put(stage, DOC + 1 + r * 8 * ROWS, ROWS, doc_rev)
            for extra in range(DOC + 2, ROWS):
                put(stage, extra + r * 8 * ROWS, ROWS, zero)

    for i in range(tiles):
        tile = step * tiles + i
        lanes = pl.ds(i * BLOCK, BLOCK)
        gated = (k_ref[0, :, lanes].astype(F32) * v_ref[0, :, lanes].astype(F32)).astype(BF16)
        weighted = (c_ref[0, :, lanes].astype(F32) * q_ref[0, :, lanes].astype(F32)).astype(BF16)
        put(stage, tile, ROWS, dot_nt(eye, gated))
        put(stage, OWN + tile, ROWS, dot_nt(eye, dot(rev, weighted).astype(BF16)))

    @pl.when(step == pl.num_programs(0) - 1)
    def _():
        copy.wait()
        for i in range(2):
            put(stage, FILT + i, ROWS, dot_nt(eye, filt[:, i * BLOCK : (i + 1) * BLOCK].astype(BF16)))
        out_ref[...] = stage[...].reshape(PEERS, ROWS, BLOCK).astype(BF16)


def conv_kernel(in_ref, out_ref, src, dst, mask, rel, rel_t, keep, stack, extra, taps, cross):
    row, col = iota(0), iota(1)
    far = ROWS * BLOCKS
    src[...] = in_ref[...].astype(F32).reshape(PEERS * ROWS, BLOCK)
    dst[...] = jnp.zeros_like(dst)
    stack[...] = jnp.zeros_like(stack)
    cross[:, BLOCKS * BLOCK :] = jnp.zeros((BLOCK, BLOCK), F32)

    def blocks(line, backward=False):
        order = range(BLOCKS - 1, -1, -1) if backward else range(BLOCKS)
        return jnp.concatenate([src[pl.ds(b * ROWS + line, 8, stride=far), :] for b in order], axis=0)

    for way, doc in enumerate((blocks(DOC), blocks(DOC + 1, True))):
        head = jnp.broadcast_to(doc[:, :1], (BLOCK, BLOCK))
        for d in range(BLOCKS):
            same = (doc[: BLOCK - 8 * d] == head[8 * d :]).astype(F32)
            if d:
                same = jnp.concatenate([jnp.zeros((8 * d, BLOCK), F32), same], axis=0)
            mask[way * BLOCK : (way + 1) * BLOCK, d * BLOCK : (d + 1) * BLOCK] = same.astype(BF16)
        for k in range(DOCS):
            at = (jnp.abs(doc - head) == k).astype(F32)
            keep[k, way * BLOCK : (way + 1) * BLOCK, :] = at
            rel[k, way * BLOCK : (way + 1) * BLOCK, :] = at.astype(BF16)
    doc, flipped = blocks(DOC), blocks(DOC + 1)
    head = jnp.broadcast_to(doc[:, :1], (BLOCK, BLOCK))
    for k in range(DOCS):
        rel_t[k] = jnp.transpose((flipped - head == k).astype(F32)).astype(BF16)

    def channel(t, carry):
        wn = blocks(OWN + t)
        for way, signal in enumerate((blocks(t), blocks(OWN + t, True))):
            even = signal.astype(BF16)
            odd = jnp.concatenate([jnp.zeros((8, BLOCK), F32), signal[: BLOCK - 8]], axis=0).astype(BF16)
            for d in range(BLOCKS):
                down = d // 2 * 16
                at = (slice(way * BLOCK + down, (way + 1) * BLOCK), slice(d * BLOCK, (d + 1) * BLOCK))
                stack[at] = (odd if d % 2 else even)[: BLOCK - down] * mask[at]
            for k in range(1, DOCS):
                extra[k, way * BLOCK : (way + 1) * BLOCK, :] = even * rel[k, way * BLOCK : (way + 1) * BLOCK, :]
        line = (t // 2) * far + FILT + t % 2
        before = jnp.zeros((BLOCK, BLOCK), F32)
        for d in range(BLOCKS):
            lags = jnp.broadcast_to(src[pl.ds(line + d * ROWS, 1), :], (BLOCK, BLOCK))
            turned = pltpu.roll(lags, 0, 1, stride=1, stride_axis=0)
            taps[d * BLOCK : (d + 1) * BLOCK, :] = jnp.where(col >= row, turned, before).astype(BF16)
            before = turned
        out = keep[0] * dot(stack[...], taps[...])
        for k in range(1, DOCS):
            out = out + keep[k] * dot(extra[k], taps[:BLOCK])
        for b in range(BLOCKS):
            dst[pl.ds(b * ROWS + t, 8, stride=far), :] = out[8 * b : 8 * b + 8]
            dst[pl.ds((BLOCKS - 1 - b) * ROWS + OWN + t, 8, stride=far), :] = out[BLOCK + 8 * b : BLOCK + 8 * b + 8]
        wt = jnp.transpose(wn).astype(BF16)
        cross[:, : BLOCKS * BLOCK] = dot(wt * rel_t[0], stack[:BLOCK, :])
        for k in range(1, DOCS):
            cross[:, :BLOCK] += dot(wt * rel_t[k], extra[k, :BLOCK, :])
        sums = []
        for d in range(BLOCKS):
            here = cross[:, d * BLOCK : (d + 1) * BLOCK]
            there = cross[:, (d + 1) * BLOCK : (d + 2) * BLOCK]
            lined = jnp.where(row + col <= BLOCK - 1, here, there)
            sums.append(jnp.sum(pltpu.roll(lined, 1, 1, stride=1, stride_axis=0), axis=0, keepdims=True))
        grad = jnp.concatenate(sums, axis=0)
        high = grad.astype(BF16).astype(F32)
        put(dst, line, ROWS, high)
        put(dst, line + 2, ROWS, grad - high)
        return carry

    lax.fori_loop(0, OWN, channel, 0)
    out_ref[...] = dst[...].reshape(PEERS, ROWS, BLOCK).astype(BF16)


def finish_kernel(q_ref, k_ref, v_ref, c_ref, in_ref, ho_ref, gq_ref, gk_ref, gv_ref, gf_ref, stage):
    step = pl.program_id(0)
    tiles = q_ref.shape[2] // BLOCK
    eye, rev = eye_rev()

    @pl.when(step == 0)
    def _():
        stage[...] = in_ref[...].astype(F32).reshape(PEERS * ROWS, BLOCK)
        turn = ((iota(0) + iota(1)) % BLOCK == 0).astype(F32).astype(BF16)
        for i in range(2):
            high = take(stage, FILT + i, ROWS, PEERS).astype(BF16)
            low = take(stage, FILT + 2 + i, ROWS, PEERS).astype(BF16)
            gf_ref[:, i * BLOCK : (i + 1) * BLOCK] = dot_nt(turn, high) + dot_nt(turn, low)

    for i in range(tiles):
        tile = step * tiles + i
        lanes = pl.ds(i * BLOCK, BLOCK)
        conv = dot_nt(eye, take(stage, tile, ROWS, PEERS).astype(BF16))
        grad = dot_nt(rev, take(stage, OWN + tile, ROWS, PEERS).astype(BF16))
        ho_ref[0, :, lanes] = (q_ref[0, :, lanes].astype(F32) * conv).astype(BF16)
        gq_ref[0, :, lanes] = (c_ref[0, :, lanes].astype(F32) * conv).astype(BF16)
        gk_ref[0, :, lanes] = (grad * v_ref[0, :, lanes].astype(F32)).astype(BF16)
        gv_ref[0, :, lanes] = (grad * k_ref[0, :, lanes].astype(F32)).astype(BF16)


def body(queries, keys, values, cotangent, doc_lengths, filter_taps):
    width = 512
    steps = queries.shape[2] // width
    tile = pl.BlockSpec((1, BLOCK, width), lambda i: (0, 0, i))
    whole = pl.BlockSpec((PEERS, ROWS, BLOCK), lambda i: (0, 0, 0))
    message = jax.ShapeDtypeStruct((PEERS, ROWS, BLOCK), BF16)
    params = pltpu.CompilerParams(vmem_limit_bytes=32 << 20)
    packed = pl.pallas_call(
        pack_kernel,
        grid=(steps,),
        in_specs=[pl.BlockSpec(memory_space=pltpu.SMEM), tile, tile, tile, tile, pl.BlockSpec(memory_space=pl.ANY)],
        out_specs=whole,
        out_shape=message,
        scratch_shapes=[
            pltpu.VMEM((PEERS * ROWS, BLOCK), F32),
            pltpu.VMEM((BLOCK, 2 * BLOCK), F32),
            pltpu.SemaphoreType.DMA,
        ],
        compiler_params=params,
        name="pack",
    )(doc_lengths, queries, keys, values, cotangent, filter_taps)
    arrived = lax.all_to_all(packed, ("dp", "ctx"), 0, 0, tiled=True)
    results = pl.pallas_call(
        conv_kernel,
        in_specs=[pl.BlockSpec(memory_space=pltpu.VMEM)],
        out_specs=pl.BlockSpec(memory_space=pltpu.VMEM),
        out_shape=message,
        scratch_shapes=[
            pltpu.VMEM((PEERS * ROWS, BLOCK), F32),
            pltpu.VMEM((PEERS * ROWS, BLOCK), F32),
            pltpu.VMEM((2 * BLOCK, BLOCKS * BLOCK), BF16),
            pltpu.VMEM((DOCS, 2 * BLOCK, BLOCK), BF16),
            pltpu.VMEM((DOCS, BLOCK, BLOCK), BF16),
            pltpu.VMEM((DOCS, 2 * BLOCK, BLOCK), F32),
            pltpu.VMEM((2 * BLOCK, BLOCKS * BLOCK), BF16),
            pltpu.VMEM((DOCS, 2 * BLOCK, BLOCK), BF16),
            pltpu.VMEM((BLOCKS * BLOCK, BLOCK), BF16),
            pltpu.VMEM((BLOCK, (BLOCKS + 1) * BLOCK), F32),
        ],
        compiler_params=params,
        name="conv",
    )(arrived)
    returned = lax.all_to_all(results, ("dp", "ctx"), 0, 0, tiled=True)
    row_out = jax.ShapeDtypeStruct(queries.shape, BF16)
    return pl.pallas_call(
        finish_kernel,
        grid=(steps,),
        in_specs=[tile, tile, tile, tile, whole],
        out_specs=[tile, tile, tile, tile, pl.BlockSpec((BLOCK, 2 * BLOCK), lambda i: (0, 0))],
        out_shape=[row_out, row_out, row_out, row_out, jax.ShapeDtypeStruct((BLOCK, 2 * BLOCK), F32)],
        scratch_shapes=[pltpu.VMEM((PEERS * ROWS, BLOCK), F32)],
        compiler_params=params,
        name="finish",
    )(queries, keys, values, cotangent, returned)


def solution(mesh):
    rows = P("dp", "ctx", None)
    return jax.shard_map(
        body,
        mesh=mesh,
        in_specs=(rows, rows, rows, rows, P("dp", None), P("ctx", None)),
        out_specs=(rows, rows, rows, rows, P("ctx", "dp")),
        check_vma=False,
    )
```

```python
import functools

import jax
import jax.numpy as jnp
from jax import lax
from jax.experimental import pallas as pl
from jax.experimental.pallas import tpu as pltpu
from jax.sharding import PartitionSpec as P

BLOCK = 128
SEQS = 8
BLOCKS = 16
PEERS = SEQS * BLOCKS
OWN = 16
DOCS = 4
ROWS = 40
FILT, DOC = 2 * OWN, 2 * OWN + 2
F32, BF16 = jnp.float32, jnp.bfloat16


def iota(axis, shape=(BLOCK, BLOCK)):
    return lax.broadcasted_iota(jnp.int32, shape, axis)


def dot(a, b):
    return jnp.dot(a, b, preferred_element_type=F32)


def dot_nt(a, b):
    return lax.dot_general(a, b, (((1,), (1,)), ((), ())), preferred_element_type=F32)


def dot_tn(a, b):
    return lax.dot_general(a, b, (((0,), (0,)), ((), ())), preferred_element_type=F32)


def eye_rev():
    row, col = iota(0), iota(1)
    return (row == col).astype(F32).astype(BF16), (row + col == BLOCK - 1).astype(F32).astype(BF16)


def put(ref, start, stride, tile):
    for r in range(tile.shape[0] // 8):
        ref[pl.ds(start + r * 8 * stride, 8, stride=stride), :] = tile[8 * r : 8 * r + 8]


def take(ref, start, stride, rows):
    return jnp.concatenate(
        [ref[pl.ds(start + r * 8 * stride, 8, stride=stride), :] for r in range(rows // 8)], axis=0
    )


def pack_kernel(len_ref, q_ref, k_ref, v_ref, c_ref, filt_hbm, out_ref, stage, filt, sem):
    step = pl.program_id(0)
    tiles = q_ref.shape[2] // BLOCK
    eye, rev = eye_rev()
    copy = pltpu.make_async_copy(
        filt_hbm.at[:, pl.ds(pl.multiple_of(lax.axis_index("dp") * 2 * BLOCK, BLOCK), 2 * BLOCK)],
        filt,
        sem,
    )

    @pl.when(step == 0)
    def _():
        copy.start()
        lane = iota(1, (8, BLOCK))
        pos = lax.axis_index("ctx") * BLOCK + lane
        pos_rev = lax.axis_index("ctx") * BLOCK + BLOCK - 1 - lane
        doc = jnp.zeros((8, BLOCK), F32)
        doc_rev = jnp.zeros((8, BLOCK), F32)
        end = jnp.int32(0)
        for i in range(DOCS):
            end = end + len_ref[0, i]
            doc = doc + (end <= pos).astype(F32)
            doc_rev = doc_rev + (end <= pos_rev).astype(F32)
        zero = jnp.zeros((8, BLOCK), F32)
        for r in range(PEERS // 8):
            put(stage, DOC + r * 8 * ROWS, ROWS, doc)
            put(stage, DOC + 1 + r * 8 * ROWS, ROWS, doc_rev)
            for extra in range(DOC + 2, ROWS):
                put(stage, extra + r * 8 * ROWS, ROWS, zero)

    gated = dot_tn((k_ref[0].astype(F32) * v_ref[0].astype(F32)).astype(BF16), eye)
    weighted = dot_tn((c_ref[0].astype(F32) * q_ref[0].astype(F32)).astype(BF16), rev)
    for i in range(tiles):
        part = slice(i * BLOCK, (i + 1) * BLOCK)
        put(stage, step * tiles + i, ROWS, gated[part])
        put(stage, OWN + step * tiles + i, ROWS, weighted[part])

    @pl.when(step == pl.num_programs(0) - 1)
    def _():
        copy.wait()
        lags = dot_tn(filt[...].astype(BF16), eye)
        for i in range(2):
            put(stage, FILT + i, ROWS, lags[i * BLOCK : (i + 1) * BLOCK])
        out_ref[...] = stage[...].reshape(PEERS, ROWS, BLOCK).astype(BF16)


def conv_kernel(in_ref, out_ref, src, dst, mask, rel, rel_t, keep, stack, extra, taps, cross, fold):
    row, col = iota(0), iota(1)
    far = ROWS * BLOCKS
    src[...] = in_ref[...].astype(F32).reshape(PEERS * ROWS, BLOCK)
    dst[...] = jnp.zeros_like(dst)
    stack[...] = jnp.zeros_like(stack)
    cross[...] = jnp.zeros_like(cross)

    def blocks(line, backward=False):
        order = range(BLOCKS - 1, -1, -1) if backward else range(BLOCKS)
        return jnp.concatenate([src[pl.ds(b * ROWS + line, 8, stride=far), :] for b in order], axis=0)

    for way, doc in enumerate((blocks(DOC), blocks(DOC + 1, True))):
        head = jnp.broadcast_to(doc[:, :1], (BLOCK, BLOCK))
        for d in range(BLOCKS):
            same = (doc[: BLOCK - 8 * d] == head[8 * d :]).astype(F32)
            if d:
                same = jnp.concatenate([jnp.zeros((8 * d, BLOCK), F32), same], axis=0)
            mask[way * BLOCK : (way + 1) * BLOCK, d * BLOCK : (d + 1) * BLOCK] = same.astype(BF16)
        for k in range(DOCS):
            at = (jnp.abs(doc - head) == k).astype(F32)
            keep[k, way * BLOCK : (way + 1) * BLOCK, :] = at
            rel[k, way * BLOCK : (way + 1) * BLOCK, :] = at.astype(BF16)
    doc, flipped = blocks(DOC), blocks(DOC + 1)
    head = jnp.broadcast_to(doc[:, :1], (BLOCK, BLOCK))
    for k in range(DOCS):
        rel_t[k] = jnp.transpose((flipped - head == k).astype(F32)).astype(BF16)

    def build(t, slot):
        for way, signal in enumerate((blocks(t), blocks(OWN + t, True))):
            even = signal.astype(BF16)
            odd = jnp.concatenate([jnp.zeros((8, BLOCK), F32), signal[: BLOCK - 8]], axis=0).astype(BF16)
            for d in range(BLOCKS):
                down = d // 2 * 16
                at = (slice(way * BLOCK + down, (way + 1) * BLOCK), slice(d * BLOCK, (d + 1) * BLOCK))
                stack[(slot,) + at] = (odd if d % 2 else even)[: BLOCK - down] * mask[at]
            for k in range(1, DOCS):
                extra[slot, k, way * BLOCK : (way + 1) * BLOCK, :] = even * rel[k, way * BLOCK : (way + 1) * BLOCK, :]
        line = (t // 2) * far + FILT + t % 2
        before = jnp.zeros((BLOCK, BLOCK), BF16)
        for d in range(BLOCKS):
            lags = jnp.broadcast_to(src[pl.ds(line + d * ROWS, 1), :], (BLOCK, BLOCK)).astype(BF16)
            turned = pltpu.roll(lags, 0, 1, stride=1, stride_axis=0)
            taps[slot, d * BLOCK : (d + 1) * BLOCK, :] = jnp.where(col >= row, turned, before)
            before = turned

    def multiply(t, slot):
        out = keep[0] * dot(stack[slot], taps[slot])
        for k in range(1, DOCS):
            out = out + keep[k] * dot(extra[slot, k], taps[slot, :BLOCK])
        for b in range(BLOCKS):
            dst[pl.ds(b * ROWS + t, 8, stride=far), :] = out[8 * b : 8 * b + 8]
            dst[pl.ds((BLOCKS - 1 - b) * ROWS + OWN + t, 8, stride=far), :] = out[BLOCK + 8 * b : BLOCK + 8 * b + 8]
        wt = jnp.transpose(blocks(OWN + t)).astype(BF16)
        cross[slot, :, : BLOCKS * BLOCK] = dot(wt * rel_t[0], stack[slot, :BLOCK, :])
        for k in range(1, DOCS):
            cross[slot, :, :BLOCK] += dot(wt * rel_t[k], extra[slot, k, :BLOCK, :])

    def gather(t, slot):
        line = (t // 2) * far + FILT + t % 2
        sums = [jnp.zeros((8, BLOCK), F32)] * BLOCKS
        for k in range(BLOCK // 8):
            part = slice(8 * k, 8 * k + 8)
            lower = 8 * k + iota(0, (8, BLOCK)) + iota(1, (8, BLOCK)) <= BLOCK - 1
            here = cross[slot, part, :BLOCK]
            for d in range(BLOCKS):
                there = cross[slot, part, (d + 1) * BLOCK : (d + 2) * BLOCK]
                sums[d] += pltpu.roll(jnp.where(lower, here, there), 8 * k + 1, 1, stride=1, stride_axis=0)
                here = there
        for d in range(BLOCKS):
            fold[slot, 8 * d : 8 * d + 8, :] = sums[d]
        grad = sum(fold[slot, pl.ds(i, BLOCKS, stride=8), :] for i in range(8))
        high = grad.astype(BF16).astype(F32)
        put(dst, line, ROWS, high)
        put(dst, line + 2, ROWS, grad - high)

    build(0, 0)

    def pair(u, carry):
        t = 2 * u
        multiply(t, 0)
        build(t + 1, 1)
        gather(jnp.maximum(t - 1, 0), 1)
        multiply(t + 1, 1)
        build(jnp.minimum(t + 2, OWN - 1), 0)
        gather(t, 0)
        return carry

    lax.fori_loop(0, OWN // 2, pair, 0)
    gather(OWN - 1, 1)
    out_ref[...] = dst[...].reshape(PEERS, ROWS, BLOCK).astype(BF16)


def finish_kernel(q_ref, k_ref, v_ref, c_ref, in_ref, ho_ref, gq_ref, gk_ref, gv_ref, gf_ref, stage):
    step = pl.program_id(0)
    tiles = q_ref.shape[2] // BLOCK
    eye, rev = eye_rev()

    @pl.when(step == 0)
    def _():
        stage[...] = in_ref[...].astype(F32).reshape(PEERS * ROWS, BLOCK)
        turn = ((iota(0) + iota(1)) % BLOCK == 0).astype(F32).astype(BF16)
        for i in range(2):
            high = take(stage, FILT + i, ROWS, PEERS).astype(BF16)
            low = take(stage, FILT + 2 + i, ROWS, PEERS).astype(BF16)
            gf_ref[:, i * BLOCK : (i + 1) * BLOCK] = dot_nt(turn, high) + dot_nt(turn, low)

    def rows(first):
        return jnp.concatenate(
            [take(stage, first + step * tiles + i, ROWS, PEERS).astype(BF16) for i in range(tiles)], axis=0
        )

    conv = dot_nt(eye, rows(0))
    grad = dot_nt(rev, rows(OWN))
    ho_ref[0] = (q_ref[0].astype(F32) * conv).astype(BF16)
    gq_ref[0] = (c_ref[0].astype(F32) * conv).astype(BF16)
    gk_ref[0] = (grad * v_ref[0].astype(F32)).astype(BF16)
    gv_ref[0] = (grad * k_ref[0].astype(F32)).astype(BF16)


def body(queries, keys, values, cotangent, doc_lengths, filter_taps):
    width = 512
    steps = queries.shape[2] // width
    tile = pl.BlockSpec((1, BLOCK, width), lambda i: (0, 0, i))
    whole = pl.BlockSpec((PEERS, ROWS, BLOCK), lambda i: (0, 0, 0))
    message = jax.ShapeDtypeStruct((PEERS, ROWS, BLOCK), BF16)
    params = pltpu.CompilerParams(vmem_limit_bytes=32 << 20)
    packed = pl.pallas_call(
        pack_kernel,
        grid=(steps,),
        in_specs=[pl.BlockSpec(memory_space=pltpu.SMEM), tile, tile, tile, tile, pl.BlockSpec(memory_space=pl.ANY)],
        out_specs=whole,
        out_shape=message,
        scratch_shapes=[
            pltpu.VMEM((PEERS * ROWS, BLOCK), F32),
            pltpu.VMEM((BLOCK, 2 * BLOCK), F32),
            pltpu.SemaphoreType.DMA,
        ],
        compiler_params=pltpu.CompilerParams(vmem_limit_bytes=60 << 20),
        name="pack",
    )(doc_lengths, queries, keys, values, cotangent, filter_taps)
    arrived = lax.all_to_all(packed, ("dp", "ctx"), 0, 0, tiled=True)
    results = pl.pallas_call(
        conv_kernel,
        in_specs=[pl.BlockSpec(memory_space=pltpu.VMEM)],
        out_specs=pl.BlockSpec(memory_space=pltpu.VMEM),
        out_shape=message,
        scratch_shapes=[
            pltpu.VMEM((PEERS * ROWS, BLOCK), F32),
            pltpu.VMEM((PEERS * ROWS, BLOCK), F32),
            pltpu.VMEM((2 * BLOCK, BLOCKS * BLOCK), BF16),
            pltpu.VMEM((DOCS, 2 * BLOCK, BLOCK), BF16),
            pltpu.VMEM((DOCS, BLOCK, BLOCK), BF16),
            pltpu.VMEM((DOCS, 2 * BLOCK, BLOCK), F32),
            pltpu.VMEM((2, 2 * BLOCK, BLOCKS * BLOCK), BF16),
            pltpu.VMEM((2, DOCS, 2 * BLOCK, BLOCK), BF16),
            pltpu.VMEM((2, BLOCKS * BLOCK, BLOCK), BF16),
            pltpu.VMEM((2, BLOCK, (BLOCKS + 1) * BLOCK), F32),
            pltpu.VMEM((2, BLOCK, BLOCK), F32),
        ],
        compiler_params=params,
        name="conv",
    )(arrived)
    returned = lax.all_to_all(results, ("dp", "ctx"), 0, 0, tiled=True)
    row_out = jax.ShapeDtypeStruct(queries.shape, BF16)
    return pl.pallas_call(
        finish_kernel,
        grid=(steps,),
        in_specs=[tile, tile, tile, tile, whole],
        out_specs=[tile, tile, tile, tile, pl.BlockSpec((BLOCK, 2 * BLOCK), lambda i: (0, 0))],
        out_shape=[row_out, row_out, row_out, row_out, jax.ShapeDtypeStruct((BLOCK, 2 * BLOCK), F32)],
        scratch_shapes=[pltpu.VMEM((PEERS * ROWS, BLOCK), F32)],
        compiler_params=params,
        name="finish",
    )(queries, keys, values, cotangent, returned)


def solution(mesh):
    rows = P("dp", "ctx", None)
    return jax.shard_map(
        body,
        mesh=mesh,
        in_specs=(rows, rows, rows, rows, P("dp", None), P("ctx", None)),
        out_specs=(rows, rows, rows, rows, P("ctx", "dp")),
        check_vma=False,
    )
```

```python
import functools

import jax
import jax.numpy as jnp
from jax import lax
from jax.experimental import pallas as pl
from jax.experimental.pallas import tpu as pltpu
from jax.sharding import PartitionSpec as P

BLOCK = 128
SEQS = 8
BLOCKS = 16
PEERS = SEQS * BLOCKS
OWN = 16
DOCS = 4
ROWS = 40
PITCH = ROWS + 1
FAR = ROWS * BLOCKS + 1
FILT, DOC = 2 * OWN, 2 * OWN + 2
F32, BF16 = jnp.float32, jnp.bfloat16


def iota(axis, shape=(BLOCK, BLOCK)):
    return lax.broadcasted_iota(jnp.int32, shape, axis)


def dot(a, b):
    return jnp.dot(a, b, preferred_element_type=F32)


def dot_nt(a, b):
    return lax.dot_general(a, b, (((1,), (1,)), ((), ())), preferred_element_type=F32)


def dot_tn(a, b):
    return lax.dot_general(a, b, (((0,), (0,)), ((), ())), preferred_element_type=F32)


def eye_rev():
    row, col = iota(0), iota(1)
    return (row == col).astype(F32).astype(BF16), (row + col == BLOCK - 1).astype(F32).astype(BF16)


def put(ref, start, stride, tile):
    for r in range(tile.shape[0] // 8):
        ref[pl.ds(start + r * 8 * stride, 8, stride=stride), :] = tile[8 * r : 8 * r + 8]


def take(ref, start, stride, rows):
    return jnp.concatenate(
        [ref[pl.ds(start + r * 8 * stride, 8, stride=stride), :] for r in range(rows // 8)], axis=0
    )


def pack_kernel(len_ref, q_ref, k_ref, v_ref, c_ref, filt_hbm, out_ref, stage, filt, sem):
    step = pl.program_id(0)
    tiles = q_ref.shape[2] // BLOCK
    eye, rev = eye_rev()
    copy = pltpu.make_async_copy(
        filt_hbm.at[:, pl.ds(pl.multiple_of(lax.axis_index("dp") * 2 * BLOCK, BLOCK), 2 * BLOCK)],
        filt,
        sem,
    )

    @pl.when(step == 0)
    def _():
        copy.start()
        lane = iota(1, (8, BLOCK))
        pos = lax.axis_index("ctx") * BLOCK + lane
        pos_rev = lax.axis_index("ctx") * BLOCK + BLOCK - 1 - lane
        doc = jnp.zeros((8, BLOCK), F32)
        doc_rev = jnp.zeros((8, BLOCK), F32)
        end = jnp.int32(0)
        for i in range(DOCS):
            end = end + len_ref[0, i]
            doc = doc + (end <= pos).astype(F32)
            doc_rev = doc_rev + (end <= pos_rev).astype(F32)
        for r in range(PEERS // 8):
            put(stage, DOC + r * 8 * PITCH, PITCH, doc)
            put(stage, DOC + 1 + r * 8 * PITCH, PITCH, doc_rev)

    gated = dot_tn((k_ref[0].astype(F32) * v_ref[0].astype(F32)).astype(BF16), eye)
    weighted = dot_tn((c_ref[0].astype(F32) * q_ref[0].astype(F32)).astype(BF16), rev)
    for i in range(tiles):
        part = slice(i * BLOCK, (i + 1) * BLOCK)
        put(stage, step * tiles + i, PITCH, gated[part])
        put(stage, OWN + step * tiles + i, PITCH, weighted[part])

    @pl.when(step == pl.num_programs(0) - 1)
    def _():
        copy.wait()
        lags = dot_tn(filt[...].astype(BF16), eye)
        for i in range(2):
            put(stage, FILT + i, PITCH, lags[i * BLOCK : (i + 1) * BLOCK])
        for r in range(PEERS):
            out_ref[r] = stage[r * PITCH : r * PITCH + ROWS, :].astype(BF16)


def conv_kernel(in_ref, out_ref, src, dst, mask, rel, rel_t, keep, stack, extra, taps, cross, fold):
    row, col = iota(0), iota(1)
    far = FAR
    for i in range(SEQS):
        src[i * FAR : i * FAR + FAR - 1, :] = (
            in_ref[i * BLOCKS : (i + 1) * BLOCKS].astype(F32).reshape(FAR - 1, BLOCK)
        )
    stack[...] = jnp.zeros_like(stack)
    cross[...] = jnp.zeros_like(cross)

    def blocks(line, backward=False):
        order = range(BLOCKS - 1, -1, -1) if backward else range(BLOCKS)
        return jnp.concatenate([src[pl.ds(b * ROWS + line, 8, stride=far), :] for b in order], axis=0)

    for way, doc in enumerate((blocks(DOC), blocks(DOC + 1, True))):
        head = jnp.broadcast_to(doc[:, :1], (BLOCK, BLOCK))
        for d in range(BLOCKS):
            same = (doc[: BLOCK - 8 * d] == head[8 * d :]).astype(F32)
            if d:
                same = jnp.concatenate([jnp.zeros((8 * d, BLOCK), F32), same], axis=0)
            mask[way * BLOCK : (way + 1) * BLOCK, d * BLOCK : (d + 1) * BLOCK] = same.astype(BF16)
        for k in range(DOCS):
            at = (jnp.abs(doc - head) == k).astype(F32)
            keep[k, way * BLOCK : (way + 1) * BLOCK, :] = at
            rel[k, way * BLOCK : (way + 1) * BLOCK, :] = at.astype(BF16)
    doc, flipped = blocks(DOC), blocks(DOC + 1)
    head = jnp.broadcast_to(doc[:, :1], (BLOCK, BLOCK))
    for k in range(DOCS):
        rel_t[k] = jnp.transpose((flipped - head == k).astype(F32)).astype(BF16)

    def build(t, slot):
        for way, signal in enumerate((blocks(t), blocks(OWN + t, True))):
            even = signal.astype(BF16)
            odd = jnp.concatenate([jnp.zeros((8, BLOCK), F32), signal[: BLOCK - 8]], axis=0).astype(BF16)
            for d in range(BLOCKS):
                down = d // 2 * 16
                at = (slice(way * BLOCK + down, (way + 1) * BLOCK), slice(d * BLOCK, (d + 1) * BLOCK))
                stack[(slot,) + at] = (odd if d % 2 else even)[: BLOCK - down] * mask[at]
            for k in range(1, DOCS):
                extra[slot, k, way * BLOCK : (way + 1) * BLOCK, :] = even * rel[k, way * BLOCK : (way + 1) * BLOCK, :]
        line = (t // 2) * far + FILT + t % 2
        before = jnp.zeros((BLOCK, BLOCK), BF16)
        for d in range(BLOCKS):
            lags = jnp.broadcast_to(src[pl.ds(line + d * ROWS, 1), :], (BLOCK, BLOCK)).astype(BF16)
            turned = pltpu.roll(lags, 0, 1, stride=1, stride_axis=0)
            taps[slot, d * BLOCK : (d + 1) * BLOCK, :] = jnp.where(col >= row, turned, before)
            before = turned

    def multiply(t, slot):
        parts = []
        for g in range(4):
            lanes = slice(512 * g, 512 * g + 512)
            rows = jnp.concatenate([stack[slot, 32 * g : BLOCK, lanes], stack[slot, BLOCK + 32 * g :, lanes]], axis=0)
            parts.append(dot(rows, taps[slot, lanes, :]))
        total = []
        for way in range(2):
            for g in range(4):
                at = [way * (BLOCK - 32 * i) + 32 * (g - i) for i in range(g + 1)]
                total.append(sum(parts[i][at[i] : at[i] + 32] for i in range(g + 1)))
        out = keep[0] * jnp.concatenate(total, axis=0)
        for k in range(1, DOCS):
            out = out + keep[k] * dot(extra[slot, k], taps[slot, :BLOCK])
        for b in range(BLOCKS):
            dst[pl.ds(b * ROWS + t, 8, stride=far), :] = out[8 * b : 8 * b + 8]
            dst[pl.ds((BLOCKS - 1 - b) * ROWS + OWN + t, 8, stride=far), :] = out[BLOCK + 8 * b : BLOCK + 8 * b + 8]
        wt = jnp.transpose(blocks(OWN + t)).astype(BF16)
        heads = wt * rel_t[0]
        cross[slot, :, BLOCK : BLOCKS * BLOCK] = dot(heads, stack[slot, :BLOCK, BLOCK:])
        cross[slot, :, :BLOCK] = dot(
            jnp.concatenate([heads] + [wt * rel_t[k] for k in range(1, DOCS)], axis=1),
            jnp.concatenate([stack[slot, :BLOCK, :BLOCK]] + [extra[slot, k, :BLOCK, :] for k in range(1, DOCS)], axis=0),
        )

    def gather(t, slot):
        line = (t // 2) * far + FILT + t % 2
        sums = [jnp.zeros((8, BLOCK), F32)] * BLOCKS
        for k in range(BLOCK // 8):
            part = slice(8 * k, 8 * k + 8)
            lower = 8 * k + iota(0, (8, BLOCK)) + iota(1, (8, BLOCK)) <= BLOCK - 1
            here = cross[slot, part, :BLOCK]
            for d in range(BLOCKS):
                there = cross[slot, part, (d + 1) * BLOCK : (d + 2) * BLOCK]
                sums[d] += pltpu.roll(jnp.where(lower, here, there), 8 * k + 1, 1, stride=1, stride_axis=0)
                here = there
        for d in range(BLOCKS):
            fold[slot, 9 * d : 9 * d + 8, :] = sums[d]
        grad = sum(take(fold.at[slot], i, 9, BLOCKS) for i in range(8))
        high = grad.astype(BF16).astype(F32)
        put(dst, line, ROWS, high)
        put(dst, line + 2, ROWS, grad - high)

    build(0, 0)

    def pair(u, carry):
        t = 2 * u
        multiply(t, 0)
        build(t + 1, 1)
        gather(jnp.maximum(t - 1, 0), 1)
        multiply(t + 1, 1)
        build(jnp.minimum(t + 2, OWN - 1), 0)
        gather(t, 0)
        return carry

    lax.fori_loop(0, OWN // 2, pair, 0)
    gather(OWN - 1, 1)
    for i in range(SEQS):
        out_ref[i * BLOCKS : (i + 1) * BLOCKS] = (
            dst[i * FAR : i * FAR + FAR - 1, :].reshape(BLOCKS, ROWS, BLOCK).astype(BF16)
        )


def finish_kernel(q_ref, k_ref, v_ref, c_ref, in_ref, ho_ref, gq_ref, gk_ref, gv_ref, gf_ref, stage):
    step = pl.program_id(0)
    tiles = q_ref.shape[2] // BLOCK
    eye, rev = eye_rev()

    @pl.when(step == 0)
    def _():
        for r in range(PEERS):
            stage[r * PITCH : r * PITCH + ROWS, :] = in_ref[r].astype(F32)
        turn = ((iota(0) + iota(1)) % BLOCK == 0).astype(F32).astype(BF16)
        for i in range(2):
            high = take(stage, FILT + i, PITCH, PEERS).astype(BF16)
            low = take(stage, FILT + 2 + i, PITCH, PEERS).astype(BF16)
            gf_ref[:, i * BLOCK : (i + 1) * BLOCK] = dot_nt(turn, high) + dot_nt(turn, low)

    def rows(first):
        return jnp.concatenate(
            [take(stage, first + step * tiles + i, PITCH, PEERS).astype(BF16) for i in range(tiles)], axis=0
        )

    conv = dot_nt(eye, rows(0))
    grad = dot_nt(rev, rows(OWN))
    ho_ref[0] = (q_ref[0].astype(F32) * conv).astype(BF16)
    gq_ref[0] = (c_ref[0].astype(F32) * conv).astype(BF16)
    gk_ref[0] = (grad * v_ref[0].astype(F32)).astype(BF16)
    gv_ref[0] = (grad * k_ref[0].astype(F32)).astype(BF16)


def body(queries, keys, values, cotangent, doc_lengths, filter_taps):
    width = 512
    steps = queries.shape[2] // width
    tile = pl.BlockSpec((1, BLOCK, width), lambda i: (0, 0, i))
    whole = pl.BlockSpec((PEERS, ROWS, BLOCK), lambda i: (0, 0, 0))
    message = jax.ShapeDtypeStruct((PEERS, ROWS, BLOCK), BF16)
    params = pltpu.CompilerParams(vmem_limit_bytes=32 << 20)
    packed = pl.pallas_call(
        pack_kernel,
        grid=(steps,),
        in_specs=[pl.BlockSpec(memory_space=pltpu.SMEM), tile, tile, tile, tile, pl.BlockSpec(memory_space=pl.ANY)],
        out_specs=whole,
        out_shape=message,
        scratch_shapes=[
            pltpu.VMEM((PEERS * PITCH, BLOCK), F32),
            pltpu.VMEM((BLOCK, 2 * BLOCK), F32),
            pltpu.SemaphoreType.DMA,
        ],
        compiler_params=pltpu.CompilerParams(vmem_limit_bytes=60 << 20),
        name="pack",
    )(doc_lengths, queries, keys, values, cotangent, filter_taps)
    arrived = lax.all_to_all(packed, ("dp", "ctx"), 0, 0, tiled=True)
    results = pl.pallas_call(
        conv_kernel,
        in_specs=[pl.BlockSpec(memory_space=pltpu.VMEM)],
        out_specs=pl.BlockSpec(memory_space=pltpu.VMEM),
        out_shape=message,
        scratch_shapes=[
            pltpu.VMEM((SEQS * FAR, BLOCK), F32),
            pltpu.VMEM((SEQS * FAR, BLOCK), F32),
            pltpu.VMEM((2 * BLOCK, BLOCKS * BLOCK), BF16),
            pltpu.VMEM((DOCS, 2 * BLOCK, BLOCK), BF16),
            pltpu.VMEM((DOCS, BLOCK, BLOCK), BF16),
            pltpu.VMEM((DOCS, 2 * BLOCK, BLOCK), F32),
            pltpu.VMEM((2, 2 * BLOCK, BLOCKS * BLOCK), BF16),
            pltpu.VMEM((2, DOCS, 2 * BLOCK, BLOCK), BF16),
            pltpu.VMEM((2, BLOCKS * BLOCK, BLOCK), BF16),
            pltpu.VMEM((2, BLOCK, (BLOCKS + 1) * BLOCK), F32),
            pltpu.VMEM((2, 9 * BLOCKS, BLOCK), F32),
        ],
        compiler_params=params,
        name="conv",
    )(arrived)
    returned = lax.all_to_all(results, ("dp", "ctx"), 0, 0, tiled=True)
    row_out = jax.ShapeDtypeStruct(queries.shape, BF16)
    return pl.pallas_call(
        finish_kernel,
        grid=(steps,),
        in_specs=[tile, tile, tile, tile, whole],
        out_specs=[tile, tile, tile, tile, pl.BlockSpec((BLOCK, 2 * BLOCK), lambda i: (0, 0))],
        out_shape=[row_out, row_out, row_out, row_out, jax.ShapeDtypeStruct((BLOCK, 2 * BLOCK), F32)],
        scratch_shapes=[pltpu.VMEM((PEERS * PITCH, BLOCK), F32)],
        compiler_params=params,
        name="finish",
    )(queries, keys, values, cotangent, returned)


def solution(mesh):
    rows = P("dp", "ctx", None)
    return jax.shard_map(
        body,
        mesh=mesh,
        in_specs=(rows, rows, rows, rows, P("dp", None), P("ctx", None)),
        out_specs=(rows, rows, rows, rows, P("ctx", "dp")),
        check_vma=False,
    )
```

```python
import functools

import jax
import jax.numpy as jnp
from jax import lax
from jax.experimental import pallas as pl
from jax.experimental.pallas import tpu as pltpu
from jax.sharding import PartitionSpec as P

BLOCK = 128
SEQS = 8
BLOCKS = 16
PEERS = SEQS * BLOCKS
OWN = 16
DOCS = 4
CHUNKS = 2
ROWS = 40
PITCH = ROWS + 1
FAR = ROWS * BLOCKS + 1
FILT, DOC = 2 * OWN, 2 * OWN + 2
F32, BF16 = jnp.float32, jnp.bfloat16


def iota(axis, shape=(BLOCK, BLOCK)):
    return lax.broadcasted_iota(jnp.int32, shape, axis)


def dot(a, b):
    return jnp.dot(a, b, preferred_element_type=F32)


def dot_nt(a, b):
    return lax.dot_general(a, b, (((1,), (1,)), ((), ())), preferred_element_type=F32)


def dot_tn(a, b):
    return lax.dot_general(a, b, (((0,), (0,)), ((), ())), preferred_element_type=F32)


def eye_rev():
    row, col = iota(0), iota(1)
    return (row == col).astype(F32).astype(BF16), (row + col == BLOCK - 1).astype(F32).astype(BF16)


def put(ref, start, stride, tile):
    for r in range(tile.shape[0] // 8):
        ref[pl.ds(start + r * 8 * stride, 8, stride=stride), :] = tile[8 * r : 8 * r + 8]


def take(ref, start, stride, rows):
    return jnp.concatenate(
        [ref[pl.ds(start + r * 8 * stride, 8, stride=stride), :] for r in range(rows // 8)], axis=0
    )


def pack_kernel(len_ref, q_hbm, k_hbm, v_hbm, c_hbm, filt_hbm, out_ref, stage, held, filt, sems, filt_sem):
    width = held.shape[2] // CHUNKS
    eye, rev = eye_rev()
    copies = [
        [
            pltpu.make_async_copy(
                hbm.at[0, :, pl.ds(n * width, width)], held.at[i, :, pl.ds(n * width, width)], sems.at[n, i]
            )
            for i, hbm in enumerate((k_hbm, v_hbm, c_hbm, q_hbm))
        ]
        for n in range(CHUNKS)
    ]
    copy = pltpu.make_async_copy(
        filt_hbm.at[:, pl.ds(pl.multiple_of(lax.axis_index("dp") * 2 * BLOCK, BLOCK), 2 * BLOCK)], filt, filt_sem
    )
    for four in copies:
        for one in four:
            one.start()
    copy.start()
    lane = iota(1, (8, BLOCK))
    pos = lax.axis_index("ctx") * BLOCK + lane
    pos_rev = lax.axis_index("ctx") * BLOCK + BLOCK - 1 - lane
    doc = jnp.zeros((8, BLOCK), F32)
    doc_rev = jnp.zeros((8, BLOCK), F32)
    end = jnp.int32(0)
    for i in range(DOCS):
        end = end + len_ref[0, i]
        doc = doc + (end <= pos).astype(F32)
        doc_rev = doc_rev + (end <= pos_rev).astype(F32)
    for r in range(PEERS // 8):
        put(stage, DOC + r * 8 * PITCH, PITCH, doc)
        put(stage, DOC + 1 + r * 8 * PITCH, PITCH, doc_rev)
    for n, four in enumerate(copies):
        for one in four:
            one.wait()
        lanes = slice(n * width, (n + 1) * width)
        key, value, cot, query = (held[i, :, lanes].astype(F32) for i in range(4))
        gated = dot_tn((key * value).astype(BF16), eye)
        weighted = dot_tn((cot * query).astype(BF16), rev)
        for i in range(width // BLOCK):
            part = slice(i * BLOCK, (i + 1) * BLOCK)
            put(stage, n * (width // BLOCK) + i, PITCH, gated[part])
            put(stage, OWN + n * (width // BLOCK) + i, PITCH, weighted[part])
    copy.wait()
    lags = dot_tn(filt[...].astype(BF16), eye)
    for i in range(2):
        put(stage, FILT + i, PITCH, lags[i * BLOCK : (i + 1) * BLOCK])
    for r in range(PEERS):
        out_ref[r] = stage[r * PITCH : r * PITCH + ROWS, :].astype(BF16)


def conv_kernel(in_ref, out_ref, src, dst, mask, rel, rel_t, keep, stack, extra, taps, cross, fold):
    row, col = iota(0), iota(1)
    far = FAR
    for i in range(SEQS):
        src[i * FAR : i * FAR + FAR - 1, :] = (
            in_ref[i * BLOCKS : (i + 1) * BLOCKS].astype(F32).reshape(FAR - 1, BLOCK)
        )
    stack[...] = jnp.zeros_like(stack)
    cross[...] = jnp.zeros_like(cross)

    def blocks(line, backward=False):
        order = range(BLOCKS - 1, -1, -1) if backward else range(BLOCKS)
        return jnp.concatenate([src[pl.ds(b * ROWS + line, 8, stride=far), :] for b in order], axis=0)

    for way, doc in enumerate((blocks(DOC), blocks(DOC + 1, True))):
        head = jnp.broadcast_to(doc[:, :1], (BLOCK, BLOCK))
        for d in range(BLOCKS):
            same = (doc[: BLOCK - 8 * d] == head[8 * d :]).astype(F32)
            if d:
                same = jnp.concatenate([jnp.zeros((8 * d, BLOCK), F32), same], axis=0)
            mask[way * BLOCK : (way + 1) * BLOCK, d * BLOCK : (d + 1) * BLOCK] = same.astype(BF16)
        for k in range(DOCS):
            at = (jnp.abs(doc - head) == k).astype(F32)
            keep[k, way * BLOCK : (way + 1) * BLOCK, :] = at
            rel[k, way * BLOCK : (way + 1) * BLOCK, :] = at.astype(BF16)
    doc, flipped = blocks(DOC), blocks(DOC + 1)
    head = jnp.broadcast_to(doc[:, :1], (BLOCK, BLOCK))
    for k in range(DOCS):
        rel_t[k] = jnp.transpose((flipped - head == k).astype(F32)).astype(BF16)

    def build(t, slot):
        for way, signal in enumerate((blocks(t), blocks(OWN + t, True))):
            even = signal.astype(BF16)
            odd = jnp.concatenate([jnp.zeros((8, BLOCK), F32), signal[: BLOCK - 8]], axis=0).astype(BF16)
            for d in range(BLOCKS):
                down = d // 2 * 16
                at = (slice(way * BLOCK + down, (way + 1) * BLOCK), slice(d * BLOCK, (d + 1) * BLOCK))
                stack[(slot,) + at] = (odd if d % 2 else even)[: BLOCK - down] * mask[at]
            for k in range(1, DOCS):
                extra[slot, k, way * BLOCK : (way + 1) * BLOCK, :] = even * rel[k, way * BLOCK : (way + 1) * BLOCK, :]
        line = (t // 2) * far + FILT + t % 2
        before = jnp.zeros((BLOCK, BLOCK), BF16)
        for d in range(BLOCKS):
            lags = jnp.broadcast_to(src[pl.ds(line + d * ROWS, 1), :], (BLOCK, BLOCK)).astype(BF16)
            turned = pltpu.roll(lags, 0, 1, stride=1, stride_axis=0)
            taps[slot, d * BLOCK : (d + 1) * BLOCK, :] = jnp.where(col >= row, turned, before)
            before = turned

    def multiply(t, slot):
        parts = []
        for g in range(4):
            lanes = slice(512 * g, 512 * g + 512)
            rows = jnp.concatenate([stack[slot, 32 * g : BLOCK, lanes], stack[slot, BLOCK + 32 * g :, lanes]], axis=0)
            parts.append(dot(rows, taps[slot, lanes, :]))
        total = []
        for way in range(2):
            for g in range(4):
                at = [way * (BLOCK - 32 * i) + 32 * (g - i) for i in range(g + 1)]
                total.append(sum(parts[i][at[i] : at[i] + 32] for i in range(g + 1)))
        out = keep[0] * jnp.concatenate(total, axis=0)
        for k in range(1, DOCS):
            out = out + keep[k] * dot(extra[slot, k], taps[slot, :BLOCK])
        for b in range(BLOCKS):
            dst[pl.ds(b * ROWS + t, 8, stride=far), :] = out[8 * b : 8 * b + 8]
            dst[pl.ds((BLOCKS - 1 - b) * ROWS + OWN + t, 8, stride=far), :] = out[BLOCK + 8 * b : BLOCK + 8 * b + 8]
        wt = jnp.transpose(blocks(OWN + t)).astype(BF16)
        heads = wt * rel_t[0]
        cross[slot, :, BLOCK : BLOCKS * BLOCK] = dot(heads, stack[slot, :BLOCK, BLOCK:])
        cross[slot, :, :BLOCK] = dot(
            jnp.concatenate([heads] + [wt * rel_t[k] for k in range(1, DOCS)], axis=1),
            jnp.concatenate([stack[slot, :BLOCK, :BLOCK]] + [extra[slot, k, :BLOCK, :] for k in range(1, DOCS)], axis=0),
        )

    def gather(t, slot):
        line = (t // 2) * far + FILT + t % 2
        sums = [jnp.zeros((8, BLOCK), F32)] * BLOCKS
        for k in range(BLOCK // 8):
            part = slice(8 * k, 8 * k + 8)
            lower = 8 * k + iota(0, (8, BLOCK)) + iota(1, (8, BLOCK)) <= BLOCK - 1
            here = cross[slot, part, :BLOCK]
            for d in range(BLOCKS):
                there = cross[slot, part, (d + 1) * BLOCK : (d + 2) * BLOCK]
                sums[d] += pltpu.roll(jnp.where(lower, here, there), 8 * k + 1, 1, stride=1, stride_axis=0)
                here = there
        for d in range(BLOCKS):
            fold[slot, 9 * d : 9 * d + 8, :] = sums[d]
        grad = sum(take(fold.at[slot], i, 9, BLOCKS) for i in range(8))
        high = grad.astype(BF16).astype(F32)
        put(dst, line, ROWS, high)
        put(dst, line + 2, ROWS, grad - high)

    build(0, 0)

    def pair(u, carry):
        t = 2 * u
        gather(jnp.maximum(t - 1, 0), 1)
        multiply(t, 0)
        build(t + 1, 1)
        gather(t, 0)
        multiply(t + 1, 1)
        build(jnp.minimum(t + 2, OWN - 1), 0)
        return carry

    lax.fori_loop(0, OWN // 2, pair, 0)
    gather(OWN - 1, 1)
    for i in range(SEQS):
        out_ref[i * BLOCKS : (i + 1) * BLOCKS] = (
            dst[i * FAR : i * FAR + FAR - 1, :].reshape(BLOCKS, ROWS, BLOCK).astype(BF16)
        )


def finish_kernel(q_ref, k_ref, v_ref, c_ref, in_ref, ho_ref, gq_ref, gk_ref, gv_ref, gf_ref, stage):
    step = pl.program_id(0)
    tiles = q_ref.shape[2] // BLOCK
    eye, rev = eye_rev()

    @pl.when(step == 0)
    def _():
        for r in range(PEERS):
            stage[r * PITCH : r * PITCH + ROWS, :] = in_ref[r].astype(F32)
        turn = ((iota(0) + iota(1)) % BLOCK == 0).astype(F32).astype(BF16)
        for i in range(2):
            high = take(stage, FILT + i, PITCH, PEERS).astype(BF16)
            low = take(stage, FILT + 2 + i, PITCH, PEERS).astype(BF16)
            gf_ref[:, i * BLOCK : (i + 1) * BLOCK] = dot_nt(turn, high) + dot_nt(turn, low)

    def rows(first):
        return jnp.concatenate(
            [take(stage, first + step * tiles + i, PITCH, PEERS).astype(BF16) for i in range(tiles)], axis=0
        )

    conv = dot_nt(eye, rows(0))
    grad = dot_nt(rev, rows(OWN))
    ho_ref[0] = (q_ref[0].astype(F32) * conv).astype(BF16)
    gq_ref[0] = (c_ref[0].astype(F32) * conv).astype(BF16)
    gk_ref[0] = (grad * v_ref[0].astype(F32)).astype(BF16)
    gv_ref[0] = (grad * k_ref[0].astype(F32)).astype(BF16)


def body(queries, keys, values, cotangent, doc_lengths, filter_taps):
    width = 2048
    steps = queries.shape[2] // width
    tile = pl.BlockSpec((1, BLOCK, width), lambda i: (0, 0, i))
    whole = pl.BlockSpec((PEERS, ROWS, BLOCK), lambda i: (0, 0, 0))
    message = jax.ShapeDtypeStruct((PEERS, ROWS, BLOCK), BF16)
    params = pltpu.CompilerParams(vmem_limit_bytes=32 << 20)
    packed = pl.pallas_call(
        pack_kernel,
        in_specs=[pl.BlockSpec(memory_space=pltpu.SMEM)] + [pl.BlockSpec(memory_space=pltpu.HBM)] * 5,
        out_specs=pl.BlockSpec(memory_space=pltpu.VMEM),
        out_shape=message,
        scratch_shapes=[
            pltpu.VMEM((PEERS * PITCH, BLOCK), F32),
            pltpu.VMEM((4,) + queries.shape[1:], BF16),
            pltpu.VMEM((BLOCK, 2 * BLOCK), F32),
            pltpu.SemaphoreType.DMA((CHUNKS, 4)),
            pltpu.SemaphoreType.DMA,
        ],
        compiler_params=pltpu.CompilerParams(vmem_limit_bytes=60 << 20),
        name="pack",
    )(doc_lengths, queries, keys, values, cotangent, filter_taps)
    arrived = lax.all_to_all(packed, ("dp", "ctx"), 0, 0, tiled=True)
    results = pl.pallas_call(
        conv_kernel,
        in_specs=[pl.BlockSpec(memory_space=pltpu.VMEM)],
        out_specs=pl.BlockSpec(memory_space=pltpu.VMEM),
        out_shape=message,
        scratch_shapes=[
            pltpu.VMEM((SEQS * FAR, BLOCK), F32),
            pltpu.VMEM((SEQS * FAR, BLOCK), F32),
            pltpu.VMEM((2 * BLOCK, BLOCKS * BLOCK), BF16),
            pltpu.VMEM((DOCS, 2 * BLOCK, BLOCK), BF16),
            pltpu.VMEM((DOCS, BLOCK, BLOCK), BF16),
            pltpu.VMEM((DOCS, 2 * BLOCK, BLOCK), F32),
            pltpu.VMEM((2, 2 * BLOCK, BLOCKS * BLOCK), BF16),
            pltpu.VMEM((2, DOCS, 2 * BLOCK, BLOCK), BF16),
            pltpu.VMEM((2, BLOCKS * BLOCK, BLOCK), BF16),
            pltpu.VMEM((2, BLOCK, (BLOCKS + 1) * BLOCK), F32),
            pltpu.VMEM((2, 9 * BLOCKS, BLOCK), F32),
        ],
        compiler_params=params,
        name="conv",
    )(arrived)
    returned = lax.all_to_all(results, ("dp", "ctx"), 0, 0, tiled=True)
    row_out = jax.ShapeDtypeStruct(queries.shape, BF16)
    return pl.pallas_call(
        finish_kernel,
        grid=(steps,),
        in_specs=[tile, tile, tile, tile, whole],
        out_specs=[tile, tile, tile, tile, pl.BlockSpec((BLOCK, 2 * BLOCK), lambda i: (0, 0))],
        out_shape=[row_out, row_out, row_out, row_out, jax.ShapeDtypeStruct((BLOCK, 2 * BLOCK), F32)],
        scratch_shapes=[pltpu.VMEM((PEERS * PITCH, BLOCK), F32)],
        compiler_params=params,
        name="finish",
    )(queries, keys, values, cotangent, returned)


def solution(mesh):
    rows = P("dp", "ctx", None)
    return jax.shard_map(
        body,
        mesh=mesh,
        in_specs=(rows, rows, rows, rows, P("dp", None), P("ctx", None)),
        out_specs=(rows, rows, rows, rows, P("ctx", "dp")),
        check_vma=False,
    )
```

```python
import functools

import jax
import jax.numpy as jnp
from jax import lax
from jax.experimental import pallas as pl
from jax.experimental.pallas import tpu as pltpu
from jax.sharding import PartitionSpec as P

BLOCK = 128
SEQS = 8
BLOCKS = 16
PEERS = SEQS * BLOCKS
OWN = 16
DOCS = 4
CHUNKS = 2
ROWS = 40
PITCH = ROWS + 1
FAR = ROWS * BLOCKS + 1
FILT, DOC = 2 * OWN, 2 * OWN + 2
F32, BF16 = jnp.float32, jnp.bfloat16


def iota(axis, shape=(BLOCK, BLOCK)):
    return lax.broadcasted_iota(jnp.int32, shape, axis)


def dot(a, b):
    return jnp.dot(a, b, preferred_element_type=F32)


def dot_nt(a, b):
    return lax.dot_general(a, b, (((1,), (1,)), ((), ())), preferred_element_type=F32)


def dot_tn(a, b):
    return lax.dot_general(a, b, (((0,), (0,)), ((), ())), preferred_element_type=F32)


def eye_rev():
    row, col = iota(0), iota(1)
    return (row == col).astype(F32).astype(BF16), (row + col == BLOCK - 1).astype(F32).astype(BF16)


def put(ref, start, stride, tile):
    for r in range(tile.shape[0] // 8):
        ref[pl.ds(start + r * 8 * stride, 8, stride=stride), :] = tile[8 * r : 8 * r + 8]


def take(ref, start, stride, rows):
    return jnp.concatenate(
        [ref[pl.ds(start + r * 8 * stride, 8, stride=stride), :] for r in range(rows // 8)], axis=0
    )


def pack_kernel(len_ref, q_hbm, k_hbm, v_hbm, c_hbm, filt_hbm, out_hbm, stage, held, filt, ready, sems, filt_sem, out_sems):
    width = held.shape[2] // CHUNKS
    eye, rev = eye_rev()
    copies = [
        [
            pltpu.make_async_copy(
                hbm.at[0, :, pl.ds(n * width, width)], held.at[i, :, pl.ds(n * width, width)], sems.at[n, i]
            )
            for i, hbm in enumerate((k_hbm, v_hbm, c_hbm, q_hbm))
        ]
        for n in range(CHUNKS)
    ]
    copy = pltpu.make_async_copy(
        filt_hbm.at[:, pl.ds(pl.multiple_of(lax.axis_index("dp") * 2 * BLOCK, BLOCK), 2 * BLOCK)], filt, filt_sem
    )
    for four in copies:
        for one in four:
            one.start()
    copy.start()
    lane = iota(1, (8, BLOCK))
    pos = lax.axis_index("ctx") * BLOCK + lane
    pos_rev = lax.axis_index("ctx") * BLOCK + BLOCK - 1 - lane
    doc = jnp.zeros((8, BLOCK), F32)
    doc_rev = jnp.zeros((8, BLOCK), F32)
    end = jnp.int32(0)
    for i in range(DOCS):
        end = end + len_ref[0, i]
        doc = doc + (end <= pos).astype(F32)
        doc_rev = doc_rev + (end <= pos_rev).astype(F32)
    for r in range(PEERS // 8):
        put(stage, DOC + r * 8 * PITCH, PITCH, doc)
        put(stage, DOC + 1 + r * 8 * PITCH, PITCH, doc_rev)
    for n, four in enumerate(copies):
        for one in four:
            one.wait()
        lanes = slice(n * width, (n + 1) * width)
        key, value, cot, query = (held[i, :, lanes].astype(F32) for i in range(4))
        gated = dot_tn((key * value).astype(BF16), eye)
        weighted = dot_tn((cot * query).astype(BF16), rev)
        for i in range(width // BLOCK):
            part = slice(i * BLOCK, (i + 1) * BLOCK)
            put(stage, n * (width // BLOCK) + i, PITCH, gated[part])
            put(stage, OWN + n * (width // BLOCK) + i, PITCH, weighted[part])
    copy.wait()
    lags = dot_tn(filt[...].astype(BF16), eye)
    for i in range(2):
        put(stage, FILT + i, PITCH, lags[i * BLOCK : (i + 1) * BLOCK])
    share = PEERS // 4
    leaving = []
    for n in range(4):
        for r in range(n * share, (n + 1) * share):
            ready[r] = stage[r * PITCH : r * PITCH + ROWS, :].astype(BF16)
        part = pl.ds(n * share, share)
        leaving.append(pltpu.make_async_copy(ready.at[part], out_hbm.at[part], out_sems.at[n]))
        leaving[n].start()
    for one in leaving:
        one.wait()


def conv_kernel(in_ref, out_ref, src, dst, mask, rel, rel_t, keep, stack, extra, taps, cross, fold):
    row, col = iota(0), iota(1)
    far = FAR
    for i in range(SEQS):
        src[i * FAR : i * FAR + FAR - 1, :] = (
            in_ref[i * BLOCKS : (i + 1) * BLOCKS].astype(F32).reshape(FAR - 1, BLOCK)
        )
    stack[...] = jnp.zeros_like(stack)
    cross[...] = jnp.zeros_like(cross)

    def blocks(line, backward=False):
        order = range(BLOCKS - 1, -1, -1) if backward else range(BLOCKS)
        return jnp.concatenate([src[pl.ds(b * ROWS + line, 8, stride=far), :] for b in order], axis=0)

    for way, doc in enumerate((blocks(DOC), blocks(DOC + 1, True))):
        head = jnp.broadcast_to(doc[:, :1], (BLOCK, BLOCK))
        for d in range(BLOCKS):
            same = (doc[: BLOCK - 8 * d] == head[8 * d :]).astype(F32)
            if d:
                same = jnp.concatenate([jnp.zeros((8 * d, BLOCK), F32), same], axis=0)
            mask[way * BLOCK : (way + 1) * BLOCK, d * BLOCK : (d + 1) * BLOCK] = same.astype(BF16)
        for k in range(DOCS):
            at = (jnp.abs(doc - head) == k).astype(F32)
            keep[k, way * BLOCK : (way + 1) * BLOCK, :] = at
            rel[k, way * BLOCK : (way + 1) * BLOCK, :] = at.astype(BF16)
    doc, flipped = blocks(DOC), blocks(DOC + 1)
    head = jnp.broadcast_to(doc[:, :1], (BLOCK, BLOCK))
    for k in range(DOCS):
        rel_t[k] = jnp.transpose((flipped - head == k).astype(F32)).astype(BF16)

    def build(t, slot):
        for way, signal in enumerate((blocks(t), blocks(OWN + t, True))):
            even = signal.astype(BF16)
            odd = jnp.concatenate([jnp.zeros((8, BLOCK), F32), signal[: BLOCK - 8]], axis=0).astype(BF16)
            for d in range(BLOCKS):
                down = d // 2 * 16
                at = (slice(way * BLOCK + down, (way + 1) * BLOCK), slice(d * BLOCK, (d + 1) * BLOCK))
                stack[(slot,) + at] = (odd if d % 2 else even)[: BLOCK - down] * mask[at]
            for k in range(1, DOCS):
                extra[slot, k, way * BLOCK : (way + 1) * BLOCK, :] = even * rel[k, way * BLOCK : (way + 1) * BLOCK, :]
        line = (t // 2) * far + FILT + t % 2
        before = jnp.zeros((BLOCK, BLOCK), BF16)
        for d in range(BLOCKS):
            lags = jnp.broadcast_to(src[pl.ds(line + d * ROWS, 1), :], (BLOCK, BLOCK)).astype(BF16)
            turned = pltpu.roll(lags, 0, 1, stride=1, stride_axis=0)
            taps[slot, d * BLOCK : (d + 1) * BLOCK, :] = jnp.where(col >= row, turned, before)
            before = turned

    def multiply(t, slot):
        parts = []
        for g in range(4):
            lanes = slice(512 * g, 512 * g + 512)
            rows = jnp.concatenate([stack[slot, 32 * g : BLOCK, lanes], stack[slot, BLOCK + 32 * g :, lanes]], axis=0)
            parts.append(dot(rows, taps[slot, lanes, :]))
        total = []
        for way in range(2):
            for g in range(4):
                at = [way * (BLOCK - 32 * i) + 32 * (g - i) for i in range(g + 1)]
                total.append(sum(parts[i][at[i] : at[i] + 32] for i in range(g + 1)))
        out = keep[0] * jnp.concatenate(total, axis=0)
        for k in range(1, DOCS):
            out = out + keep[k] * dot(extra[slot, k], taps[slot, :BLOCK])
        for b in range(BLOCKS):
            dst[pl.ds(b * ROWS + t, 8, stride=far), :] = out[8 * b : 8 * b + 8]
            dst[pl.ds((BLOCKS - 1 - b) * ROWS + OWN + t, 8, stride=far), :] = out[BLOCK + 8 * b : BLOCK + 8 * b + 8]

    def correlate(t, slot):
        wt = jnp.transpose(blocks(OWN + t)).astype(BF16)
        heads = wt * rel_t[0]
        cross[slot, :, BLOCK : BLOCKS * BLOCK] = dot(heads, stack[slot, :BLOCK, BLOCK:])
        cross[slot, :, :BLOCK] = dot(
            jnp.concatenate([heads] + [wt * rel_t[k] for k in range(1, DOCS)], axis=1),
            jnp.concatenate([stack[slot, :BLOCK, :BLOCK]] + [extra[slot, k, :BLOCK, :] for k in range(1, DOCS)], axis=0),
        )

    def gather(t, slot):
        line = (t // 2) * far + FILT + t % 2
        sums = [jnp.zeros((8, BLOCK), F32)] * BLOCKS
        for k in range(BLOCK // 8):
            part = slice(8 * k, 8 * k + 8)
            lower = 8 * k + iota(0, (8, BLOCK)) + iota(1, (8, BLOCK)) <= BLOCK - 1
            here = cross[slot, part, :BLOCK]
            for d in range(BLOCKS):
                there = cross[slot, part, (d + 1) * BLOCK : (d + 2) * BLOCK]
                sums[d] += pltpu.roll(jnp.where(lower, here, there), 8 * k + 1, 1, stride=1, stride_axis=0)
                here = there
        for d in range(BLOCKS):
            fold[slot, 9 * d : 9 * d + 8, :] = sums[d]
        grad = sum(take(fold.at[slot], i, 9, BLOCKS) for i in range(8))
        high = grad.astype(BF16).astype(F32)
        put(dst, line, ROWS, high)
        put(dst, line + 2, ROWS, grad - high)

    build(0, 0)

    def pair(u, carry):
        t = 2 * u
        multiply(t, 0)
        gather(jnp.maximum(t - 1, 0), 1)
        correlate(t, 0)
        build(t + 1, 1)
        multiply(t + 1, 1)
        gather(t, 0)
        correlate(t + 1, 1)
        build(jnp.minimum(t + 2, OWN - 1), 0)
        return carry

    lax.fori_loop(0, OWN // 2, pair, 0)
    gather(OWN - 1, 1)
    for i in range(SEQS):
        out_ref[i * BLOCKS : (i + 1) * BLOCKS] = (
            dst[i * FAR : i * FAR + FAR - 1, :].reshape(BLOCKS, ROWS, BLOCK).astype(BF16)
        )


def finish_kernel(q_ref, k_ref, v_ref, c_ref, in_ref, ho_ref, gq_ref, gk_ref, gv_ref, gf_ref, stage):
    step = pl.program_id(0)
    tiles = q_ref.shape[2] // BLOCK
    eye, rev = eye_rev()

    @pl.when(step == 0)
    def _():
        for r in range(PEERS):
            stage[r * PITCH : r * PITCH + ROWS, :] = in_ref[r].astype(F32)
        turn = ((iota(0) + iota(1)) % BLOCK == 0).astype(F32).astype(BF16)
        for i in range(2):
            high = take(stage, FILT + i, PITCH, PEERS).astype(BF16)
            low = take(stage, FILT + 2 + i, PITCH, PEERS).astype(BF16)
            gf_ref[:, i * BLOCK : (i + 1) * BLOCK] = dot_nt(turn, high) + dot_nt(turn, low)

    def rows(first):
        return jnp.concatenate(
            [take(stage, first + step * tiles + i, PITCH, PEERS).astype(BF16) for i in range(tiles)], axis=0
        )

    conv = dot_nt(eye, rows(0))
    grad = dot_nt(rev, rows(OWN))
    ho_ref[0] = (q_ref[0].astype(F32) * conv).astype(BF16)
    gq_ref[0] = (c_ref[0].astype(F32) * conv).astype(BF16)
    gk_ref[0] = (grad * v_ref[0].astype(F32)).astype(BF16)
    gv_ref[0] = (grad * k_ref[0].astype(F32)).astype(BF16)


def body(queries, keys, values, cotangent, doc_lengths, filter_taps):
    width = 2048
    steps = queries.shape[2] // width
    tile = pl.BlockSpec((1, BLOCK, width), lambda i: (0, 0, i))
    whole = pl.BlockSpec((PEERS, ROWS, BLOCK), lambda i: (0, 0, 0))
    message = jax.ShapeDtypeStruct((PEERS, ROWS, BLOCK), BF16)
    params = pltpu.CompilerParams(vmem_limit_bytes=32 << 20)
    packed = pl.pallas_call(
        pack_kernel,
        in_specs=[pl.BlockSpec(memory_space=pltpu.SMEM)] + [pl.BlockSpec(memory_space=pltpu.HBM)] * 5,
        out_specs=pl.BlockSpec(memory_space=pl.ANY),
        out_shape=message,
        scratch_shapes=[
            pltpu.VMEM((PEERS * PITCH, BLOCK), F32),
            pltpu.VMEM((4,) + queries.shape[1:], BF16),
            pltpu.VMEM((BLOCK, 2 * BLOCK), F32),
            pltpu.VMEM((PEERS, ROWS, BLOCK), BF16),
            pltpu.SemaphoreType.DMA((CHUNKS, 4)),
            pltpu.SemaphoreType.DMA,
            pltpu.SemaphoreType.DMA((4,)),
        ],
        compiler_params=pltpu.CompilerParams(vmem_limit_bytes=60 << 20),
        name="pack",
    )(doc_lengths, queries, keys, values, cotangent, filter_taps)
    arrived = lax.all_to_all(packed, ("dp", "ctx"), 0, 0, tiled=True)
    results = pl.pallas_call(
        conv_kernel,
        in_specs=[pl.BlockSpec(memory_space=pltpu.VMEM)],
        out_specs=pl.BlockSpec(memory_space=pltpu.VMEM),
        out_shape=message,
        scratch_shapes=[
            pltpu.VMEM((SEQS * FAR, BLOCK), F32),
            pltpu.VMEM((SEQS * FAR, BLOCK), F32),
            pltpu.VMEM((2 * BLOCK, BLOCKS * BLOCK), BF16),
            pltpu.VMEM((DOCS, 2 * BLOCK, BLOCK), BF16),
            pltpu.VMEM((DOCS, BLOCK, BLOCK), BF16),
            pltpu.VMEM((DOCS, 2 * BLOCK, BLOCK), F32),
            pltpu.VMEM((2, 2 * BLOCK, BLOCKS * BLOCK), BF16),
            pltpu.VMEM((2, DOCS, 2 * BLOCK, BLOCK), BF16),
            pltpu.VMEM((2, BLOCKS * BLOCK, BLOCK), BF16),
            pltpu.VMEM((2, BLOCK, (BLOCKS + 1) * BLOCK), F32),
            pltpu.VMEM((2, 9 * BLOCKS, BLOCK), F32),
        ],
        compiler_params=params,
        name="conv",
    )(arrived)
    returned = lax.all_to_all(results, ("dp", "ctx"), 0, 0, tiled=True)
    row_out = jax.ShapeDtypeStruct(queries.shape, BF16)
    return pl.pallas_call(
        finish_kernel,
        grid=(steps,),
        in_specs=[tile, tile, tile, tile, whole],
        out_specs=[tile, tile, tile, tile, pl.BlockSpec((BLOCK, 2 * BLOCK), lambda i: (0, 0))],
        out_shape=[row_out, row_out, row_out, row_out, jax.ShapeDtypeStruct((BLOCK, 2 * BLOCK), F32)],
        scratch_shapes=[pltpu.VMEM((PEERS * PITCH, BLOCK), F32)],
        compiler_params=params,
        name="finish",
    )(queries, keys, values, cotangent, returned)


def solution(mesh):
    rows = P("dp", "ctx", None)
    return jax.shard_map(
        body,
        mesh=mesh,
        in_specs=(rows, rows, rows, rows, P("dp", None), P("ctx", None)),
        out_specs=(rows, rows, rows, rows, P("ctx", "dp")),
        check_vma=False,
    )
```
